32 devices in a mesh: az: 2 (over x), rad: 4 (over y, core), ax: 4 (over z).
Axes of the slice: x: 2, y: 2, z: 4, core: 2. Of those that a mesh axis runs over, the one named last changes fastest.
Arguments:
- velocity: float32 [3, 32, 1536, 512], P(None, 'ax', 'az', 'rad'), may hold values from -40 to 40, as said below
- cutoff: int32 [512], replicated, may hold values from 2 to 511, as said below
- shells: int32 [3], replicated, may hold values from 128 to 256, as said below
Outputs:
- filtered: float32 [3, 32, 1536, 512], P(None, 'ax', 'az', 'rad')
- viscosity: float32 [32, 1536, 512], P('ax', 'az', 'rad')
- coefficient: float32 [512], P('rad')
The draws below stay inside these ranges and needn't reach their ends.
Inputs may be any that keep to these rules, and one draw needn't show every extreme that they name: `velocity`: components in the order axial, radial, azimuthal. cutoff of shell k is the highest azimuthal mode kept there; 511 is reached. `shells`: one count per velocity component; one of the three equals 256.
All inputs are finite; a program needn't handle non-finite values.
Results may differ from the reference program's by a relative error of at most 0.0003.
Values sent between devices are 32-bit elements; how exact they have to be, the bound alone decides.
A program may use at most 384 MiB of HBM per device.

```python
import math
import jax
import jax.numpy as jnp
from jax import lax

NTH = 1536
MODES = 512
NZ = 32
NR = 512
MAXSH = 256


def draw_velocity(key, part):
    subkeys = jax.random.split(key, 5)
    full_shape = (3, NZ, NTH, NR)
    rough_part = jax.random.truncated_normal(subkeys[0], -4.0, 4.0, full_shape, jnp.float32)
    azimuth_freq = jax.random.randint(subkeys[1], (3, 4), 1, 6)
    axial_freq = jax.random.randint(subkeys[2], (3, 4), 0, 3)
    strengths = jax.random.uniform(subkeys[3], (3, 4), jnp.float32, -1.0, 1.0)
    offsets = jax.random.uniform(subkeys[4], (3, 4), jnp.float32, 0.0, 2.0 * math.pi)
    azimuth_pos = jnp.arange(NTH, dtype=jnp.float32) / NTH
    axial_pos = jnp.arange(NZ, dtype=jnp.float32) / NZ
    smooth_part = jnp.zeros((3, NZ, NTH, 1), jnp.float32)
    for term_index in range(4):
        phases = 2.0 * math.pi * (azimuth_freq[:, term_index, None, None, None] * azimuth_pos[None, None, :, None] + axial_freq[:, term_index, None, None, None] * axial_pos[None, :, None, None]) + offsets[:, term_index, None, None, None]
        smooth_part = smooth_part + strengths[:, term_index, None, None, None] * jnp.cos(phases)
    mixing = 0.8 * azimuth_pos[None, None, :, None]
    amplitude = 1.0 + 2.0 * axial_pos[None, :, None, None]
    values = amplitude * ((1.0 - mixing) * rough_part + mixing * smooth_part)
    return values.astype(jnp.float32)


def draw_cutoff(key, part):
    shell_ids = jnp.arange(NR, dtype=jnp.int32)
    base_mode = (shell_ids + 1) * MODES // MAXSH
    jitter = jax.random.randint(key, (NR,), 0, 4) * (shell_ids > 0).astype(jnp.int32)
    return jnp.minimum(base_mode + jitter, MODES - 1).astype(jnp.int32)


def draw_shells(key, part):
    first_key, second_key = jax.random.split(key)
    counts = jax.random.randint(first_key, (3,), MAXSH // 2, MAXSH + 1)
    chosen = jax.random.randint(second_key, (), 0, 3)
    return jnp.where(jnp.arange(3) == chosen, MAXSH, counts).astype(jnp.int32)


def setup_inputs(seed: int = 0) -> dict:
    seeds = jax.random.split(jax.random.key(seed), 4)
    velocity = draw_velocity(jax.random.fold_in(seeds[3], 71), 0)
    cutoff = draw_cutoff(jax.random.fold_in(seeds[3], 71), 0)
    shells = draw_shells(jax.random.fold_in(seeds[3], 71), 0)
    return dict(velocity=velocity, cutoff=cutoff, shells=shells)


index_pairs = ((0, 0), (1, 1), (2, 2), (0, 1), (0, 2), (1, 2))

def spacing_of(shell_pos, azimuths):
    return jnp.maximum(shell_pos * (2.0 * math.pi / azimuths), 1.0)

def strain(source, shell_pos, spacing):
    center = source[:, 1:-1, 1:-1, 1:-1]
    along_z = (source[:, 2:, 1:-1, 1:-1] - source[:, :-2, 1:-1, 1:-1]) * 0.5
    along_t = (source[:, 1:-1, 2:, 1:-1] - source[:, 1:-1, :-2, 1:-1]) * (0.5 / spacing)
    along_r = (source[:, 1:-1, 1:-1, 2:] - source[:, 1:-1, 1:-1, :-2]) * 0.5
    tensor = jnp.stack([along_z[0], along_r[1], along_t[2] + center[1] / shell_pos, 0.5 * (along_r[0] + along_z[1]), 0.5 * (along_t[0] + along_z[2]), 0.5 * (along_r[2] - center[2] / shell_pos + along_t[1])])
    magnitude = jnp.sqrt(2.0 * lax.optimization_barrier(jnp.sum(tensor[:3] ** 2, axis=0)) + 4.0 * lax.optimization_barrier(jnp.sum(tensor[3:] ** 2, axis=0)))
    return (tensor, magnitude)

def smooth(source):
    partial_value = 0.25 * source[:, :-2] + 0.5 * source[:, 1:-1] + 0.25 * source[:, 2:]
    return 0.25 * partial_value[:, :, :-2] + 0.5 * partial_value[:, :, 1:-1] + 0.25 * partial_value[:, :, 2:]

def outer_terms(source):
    return jnp.stack([source[first] * source[second] for first, second in index_pairs])

def contract(left_side, right_side):
    return lax.optimization_barrier(jnp.sum(left_side[:3] * right_side[:3], axis=0)) + 2.0 * lax.optimization_barrier(jnp.sum(left_side[3:] * right_side[3:], axis=0))

def identity_sums(hat_products, hat_model, hat_velocity, hat_tensor, hat_magnitude, spacing):
    leonard = hat_products - outer_terms(hat_velocity)
    trace_third = (leonard[0] + leonard[1] + leonard[2]) / 3.0
    leonard = jnp.concatenate([leonard[:3] - trace_third, leonard[3:]])
    scale_sq = jnp.power(spacing, 2.0 / 3.0)
    model_tensor = 2.0 * scale_sq * (hat_model - 4.0 * hat_magnitude * hat_tensor)
    numerator = lax.optimization_barrier(jnp.sum(contract(leonard, model_tensor), axis=(0, 1)))
    denominator = lax.optimization_barrier(jnp.sum(contract(model_tensor, model_tensor), axis=(0, 1)))
    return (numerator, denominator)

def deep_terms(padded, shell_ext, shell_int, azimuths):
    spacing_ext = spacing_of(shell_ext, azimuths)
    spacing_int = spacing_of(shell_int, azimuths)
    tensor, magnitude = strain(padded, shell_ext, spacing_ext)
    center = padded[:, 1:-1, 1:-1, 2:-2]
    model_terms = magnitude[:, :, 1:-1] * tensor[:, :, :, 1:-1]
    filtered_terms = smooth(jnp.concatenate([outer_terms(center), model_terms]))
    hat_padded = smooth(padded[:, :, :, 1:-1])
    hat_tensor, hat_magnitude = strain(hat_padded, shell_int, spacing_int)
    numerator, denominator = identity_sums(filtered_terms[:6], filtered_terms[6:], hat_padded[:, 1:-1, 1:-1, 1:-1], hat_tensor, hat_magnitude, spacing_int)
    return (magnitude[1:-1, 1:-1, 1:-1], numerator, denominator)

def reference(velocity, cutoff, shells):
    planes = velocity.shape[1]
    azimuths = velocity.shape[2]
    radial = velocity.shape[3]
    wrapped = jnp.pad(velocity, ((0, 0), (2, 2), (2, 2), (0, 0)), mode='wrap')
    padded = jnp.pad(wrapped, ((0, 0), (0, 0), (0, 0), (2, 2)))

    def one_block(block_id):
        first_shell = block_id * 8
        window = lax.dynamic_slice_in_dim(padded, first_shell, 12, axis=3)
        base_shell = first_shell.astype(jnp.float32)
        shell_ext = base_shell + jnp.arange(10, dtype=jnp.float32) - 0.5
        shell_int = base_shell + jnp.arange(8, dtype=jnp.float32) + 0.5
        return deep_terms(window, shell_ext, shell_int, azimuths)
    blocks = jnp.arange(radial // 8, dtype=jnp.int32)
    magnitude, numerator, denominator = lax.map(one_block, blocks)
    magnitude = jnp.moveaxis(magnitude, 0, 2).reshape(planes, azimuths, radial)
    numerator = numerator.reshape(radial)
    denominator = denominator.reshape(radial)
    surface_cells = planes * azimuths
    coefficient = numerator / surface_cells / (denominator / surface_cells + 1e-06)
    shell_all = jnp.arange(radial, dtype=jnp.float32) + 0.5
    viscosity = coefficient * jnp.power(spacing_of(shell_all, azimuths), 2.0 / 3.0) * magnitude
    mode_ids = jnp.arange(azimuths // 2 + 1, dtype=jnp.int32)[:, None]
    shell_ids = jnp.arange(radial, dtype=jnp.int32)[None, :]
    pieces = []
    for component in range(3):
        spectrum = jnp.fft.rfft(velocity[component], axis=1)
        live_rows = shell_ids < shells[component]
        kept_modes = ((mode_ids <= cutoff[None, :]) & live_rows).astype(jnp.float32)
        rebuilt = jnp.fft.irfft(spectrum * kept_modes, n=azimuths, axis=1)
        pieces.append(jnp.where(live_rows, rebuilt, velocity[component]).astype(jnp.float32))
    filtered = jnp.stack(pieces)
    return (filtered, viscosity, coefficient)
```

```python
import functools
import math

import jax
import jax.numpy as jnp
import numpy as np
from jax import lax
from jax.experimental import pallas as pl
from jax.experimental.pallas import tpu as pltpu
from jax.sharding import PartitionSpec as P

MODES = 512
NODES = 48
PAD = 16
CHUNK = 16
F32 = jnp.float32
BF16 = jnp.bfloat16
PAIRS = ((0, 0), (1, 1), (2, 2), (0, 1), (0, 2), (1, 2))


def shift_from(block, axis, step, periodic=True):
    count = lax.axis_size(axis)
    pairs = [((i + step) % count, i) for i in range(count) if periodic or 0 <= i + step < count]
    return lax.ppermute(block, axis, pairs)


def spacing_of(shell_pos, azimuths):
    return jnp.maximum(shell_pos * (2.0 * math.pi / azimuths), 1.0)


def stencil_kernel(rows, below_ref, here_ref, above_ref, edge_ref, lane_ref,
                   mag_ref, sums_ref, prev_q, prev_h, full):
    step = pl.program_id(0)
    inv_pos = lane_ref[0:1, :]
    half_space = lane_ref[1:2, :]
    scale = lane_ref[2:3, :]
    lane = lax.broadcasted_iota(jnp.int32, (CHUNK, 128), 1)

    @pl.when(step == 0)
    def _():
        prev_q[...] = jnp.zeros_like(prev_q)
        prev_h[...] = jnp.zeros_like(prev_h)
        sums_ref[...] = jnp.zeros_like(sums_ref)

    def produce(i, carry):
        base = pl.multiple_of(i * CHUNK, 8)
        here = pl.ds(base + 8, CHUNK)
        out = pl.ds(base, CHUNK)
        v, dz, dt, dr = [], [], [], []
        for c in range(3):
            wide = here_ref[c, 0, pl.ds(base, CHUNK + 16), :]
            mid = wide[8 : 8 + CHUNK]
            edge = edge_ref[c, 0, here, :]
            v.append(mid)
            dt.append((wide[9 : 9 + CHUNK] - wide[7 : 7 + CHUNK]) * half_space)
            dz.append((above_ref[c, 0, here, :] - below_ref[c, 0, here, :]) * 0.5)
            up = jnp.where(lane == 127, edge, pltpu.roll(mid, 127, 1))
            down = jnp.where(lane == 0, edge, pltpu.roll(mid, 1, 1))
            dr.append((up - down) * 0.5)
        tensor = [
            dz[0],
            dr[1],
            dt[2] + v[1] * inv_pos,
            0.5 * (dr[0] + dz[1]),
            0.5 * (dt[0] + dz[2]),
            0.5 * (dr[2] - v[2] * inv_pos + dt[1]),
        ]
        diag = tensor[0] * tensor[0] + tensor[1] * tensor[1] + tensor[2] * tensor[2]
        off = tensor[3] * tensor[3] + tensor[4] * tensor[4] + tensor[5] * tensor[5]
        mag = jnp.sqrt(2.0 * diag + 4.0 * off)
        mag_ref[0, out, :] = mag
        fields = v + [v[a] * v[b] for a, b in PAIRS] + tensor + [mag * x for x in tensor]
        for f, q in enumerate(fields):
            h = prev_q[f, out, :] + q
            full[f, out, :] = prev_h[f, out, :] + h
            prev_q[f, out, :] = q
            prev_h[f, out, :] = h
        return carry

    lax.fori_loop(0, (rows + 16) // CHUNK, produce, 0)

    def smoothed(f, base):
        wide = full[f, pl.ds(base, CHUNK + 16), :]
        mid = wide[8 : 8 + CHUNK]
        return (wide[7 : 7 + CHUNK] + wide[9 : 9 + CHUNK] + (mid + mid)) * 0.0625

    def consume(i, carry):
        num, den = carry
        base = pl.multiple_of(i * CHUNK, 8)
        hat_v = [smoothed(c, base) for c in range(3)]
        leo = [smoothed(3 + n, base) - hat_v[a] * hat_v[b] for n, (a, b) in enumerate(PAIRS)]
        third = (leo[0] + leo[1] + leo[2]) * (1.0 / 3.0)
        leo = [x - third for x in leo[:3]] + leo[3:]
        hat_t = [smoothed(9 + n, base) for n in range(6)]
        diag = hat_t[0] * hat_t[0] + hat_t[1] * hat_t[1] + hat_t[2] * hat_t[2]
        off = hat_t[3] * hat_t[3] + hat_t[4] * hat_t[4] + hat_t[5] * hat_t[5]
        four_mag = 4.0 * jnp.sqrt(2.0 * diag + 4.0 * off)
        lm_d = lm_o = mm_d = mm_o = 0.0
        for n in range(6):
            model = (smoothed(15 + n, base) - four_mag * hat_t[n]) * scale
            lm, mm = leo[n] * model, model * model
            if n < 3:
                lm_d, mm_d = lm_d + lm, mm_d + mm
            else:
                lm_o, mm_o = lm_o + lm, mm_o + mm
        return (num + (lm_d + 2.0 * lm_o), den + (mm_d + 2.0 * mm_o))

    @pl.when(step >= 2)
    def _():
        zero = jnp.zeros((CHUNK, 128), F32)
        num, den = lax.fori_loop(0, rows // CHUNK, consume, (zero, zero))
        sums_ref[0] += num
        sums_ref[1] += den


def stencil(padded, edges, lanes):
    _, deep, tall, width = padded.shape
    rows = tall - 2 * PAD
    steps = deep - 2
    block = (3, 1, tall, width)
    return pl.pallas_call(
        functools.partial(stencil_kernel, rows),
        grid=(steps,),
        in_specs=[
            pl.BlockSpec(block, lambda j: (0, j, 0, 0)),
            pl.BlockSpec(block, lambda j: (0, j + 1, 0, 0)),
            pl.BlockSpec(block, lambda j: (0, j + 2, 0, 0)),
            pl.BlockSpec(block, lambda j: (0, j, 0, 0)),
            pl.BlockSpec((8, width), lambda j: (0, 0)),
        ],
        out_specs=[
            pl.BlockSpec((1, rows + 16, width), lambda j: (j, 0, 0)),
            pl.BlockSpec((2, CHUNK, width), lambda j: (0, 0, 0)),
        ],
        out_shape=[
            jax.ShapeDtypeStruct((steps, rows + 16, width), F32),
            jax.ShapeDtypeStruct((2, CHUNK, width), F32),
        ],
        scratch_shapes=[pltpu.VMEM((21, rows + 16, width), F32)] * 3,
        compiler_params=pltpu.CompilerParams(vmem_limit_bytes=58 * 2**20),
        cost_estimate=pl.CostEstimate(flops=10**9, bytes_accessed=10**8, transcendentals=0),
        name="stencil",
    )(padded, padded, padded, edges, lanes)


def split(x):
    high = x.astype(BF16)
    return high, (x - high.astype(F32)).astype(BF16)


def split_table(x):
    high = lax.reduce_precision(x, 8, 7)
    return high.astype(BF16), (x - high).astype(BF16)


def mm(a, b):
    return jnp.dot(a, b, preferred_element_type=F32)


def cross_tables(azimuths, parts):
    local = azimuths // parts
    pos = math.pi * (np.arange(local) - (local - 1) / 2.0) / azimuths
    edge = math.tan(math.pi * local / (2.0 * azimuths)) if parts > 1 else 1.0
    ratio = np.tan(pos) / edge
    var = np.log((1.0 + ratio) / (1.0 - ratio))
    reach = var[-1]
    theta = (np.arange(NODES) + 0.5) * math.pi / NODES
    nodes = reach * np.cos(theta)
    node_pos = np.arctan(edge * np.tanh(nodes / 2.0))
    weight = np.sin(theta) * (-1.0) ** np.arange(NODES)
    gap = var[:, None] - nodes[None, :]
    gap = np.where(np.abs(gap) < 1e-13, 1e-13, gap)
    lag = weight[None, :] / gap
    lag = lag / np.sum(lag, axis=1, keepdims=True)
    spread = lag / np.cos(pos)[:, None]
    gather = []
    for away in range(1, parts):
        source = pos + math.pi * local * away / azimuths
        gather.append(np.cos(node_pos)[:, None] / np.sin(node_pos[:, None] - source[None, :]) / azimuths)
    return spread.astype(np.float32), np.stack(gather).astype(np.float32)


def twice(x):
    return jnp.concatenate([x, x], axis=1)


def moment_kernel(x_ref, wave_ref, turn_ref, table_ref, out_ref):
    x = jnp.concatenate([x_ref[0, 0], x_ref[0, 1]], axis=1)
    c_hi, c_lo = split(x * twice(wave_ref[0]))
    s_hi, s_lo = split(x * twice(wave_ref[1]))
    for away in range(table_ref.shape[0]):
        table = table_ref[away]

        def apply(high, low):
            both = mm(table, high)
            return both[:NODES] + (both[NODES:] + mm(table[:NODES], low))

        by_cos, by_sin = apply(c_hi, c_lo), apply(s_hi, s_lo)
        cos_turn = twice(turn_ref[away, 0:1])
        sin_turn = twice(turn_ref[away, 1:2])
        first = by_cos * cos_turn - by_sin * sin_turn
        second = by_sin * cos_turn + by_cos * sin_turn
        for k in range(2):
            cols = slice(128 * k, 128 * k + 128)
            out_ref[away, 0, k, :NODES] = first[:, cols]
            out_ref[away, 0, k, NODES:] = second[:, cols]


def filter_kernel(x_ref, far_ref, live_ref, scaling_ref, wave_ref, spread_ref,
                  fwd_hi, fwd_lo, inv_hi, inv_lo, out_ref):
    x = jnp.concatenate([x_ref[0, 0], x_ref[0, 1]], axis=1)
    x_hi, x_lo = split(x)
    spectrum = mm(fwd_hi[...], x_hi) + (mm(fwd_hi[...], x_lo) + mm(fwd_lo[...], x_hi))
    s_hi, s_lo = split(spectrum * twice(scaling_ref[...]))
    near = mm(inv_hi[...], s_hi) + (mm(inv_hi[...], s_lo) + mm(inv_lo[...], s_hi))
    far = jnp.concatenate([far_ref[0, 0], far_ref[0, 1]], axis=1)
    f_hi, f_lo = split(far)

    def spread(rows):
        stacked = jnp.concatenate([f_hi[rows], f_lo[rows], f_hi[rows]], axis=0)
        return mm(spread_ref[...], stacked)

    by_cos = spread(slice(0, NODES))
    by_sin = spread(slice(NODES, 2 * NODES))
    result = near + (twice(wave_ref[1]) * by_cos - twice(wave_ref[0]) * by_sin)
    result = jnp.where(twice(live_ref[0]) > 0.5, result, x)
    out_ref[0, 0] = result[:, :128]
    out_ref[0, 1] = result[:, 128:]


def polar_tables(cutoffs, columns, azimuths):
    order = 2 * cutoffs + 1
    offset = 2 * jnp.arange(columns, dtype=jnp.int32) - (columns - 1)
    unit = math.pi / (2.0 * azimuths)
    phase = (offset[:, None] * order[None, :] % (4 * azimuths)).astype(F32) * unit
    wave = jnp.stack([jnp.cos(phase), jnp.sin(phase)])
    modes = jnp.arange(MODES, dtype=jnp.int32)
    angle = (2 * offset[None, :] * modes[:, None] % (4 * azimuths)).astype(F32) * unit
    fourier = jnp.concatenate([jnp.cos(angle), jnp.sin(angle)], axis=0)
    weight = jnp.where(modes == 0, 1.0, 2.0).astype(F32) / azimuths
    kept = jnp.where(modes[:, None] <= cutoffs[None, :], weight[:, None], 0.0)
    return wave, fourier, jnp.concatenate([kept, kept], axis=0)


def moments(velocity, wave, turn, table):
    comps, planes, columns, width = velocity.shape
    far = table.shape[0]
    return pl.pallas_call(
        moment_kernel,
        grid=(comps, planes // 2),
        in_specs=[
            pl.BlockSpec((1, 2, columns, width), lambda c, z: (c, z, 0, 0)),
            pl.BlockSpec(wave.shape, lambda c, z: (0, 0, 0)),
            pl.BlockSpec(turn.shape, lambda c, z: (0, 0, 0)),
            pl.BlockSpec(table.shape, lambda c, z: (0, 0, 0)),
        ],
        out_specs=pl.BlockSpec((far, 1, 2, 2 * NODES, width), lambda c, z: (0, c, z, 0, 0)),
        out_shape=jax.ShapeDtypeStruct((far, comps, planes, 2 * NODES, width), F32),
        name="moments",
    )(velocity, wave, turn, table)


def filtered_of(velocity, far, live, scaling, wave, spread, fourier):
    comps, planes, columns, width = velocity.shape
    fwd_hi, fwd_lo = split_table(fourier)
    tables = (fwd_hi, fwd_lo, fwd_hi.T, fwd_lo.T)

    def whole(x):
        return pl.BlockSpec(x.shape, lambda c, z: (0,) * x.ndim, pipeline_mode=pl.Buffered(1))

    block = pl.BlockSpec((1, 2, columns, width), lambda c, z: (c, z, 0, 0))
    return pl.pallas_call(
        filter_kernel,
        grid=(comps, planes // 2),
        in_specs=[
            block,
            pl.BlockSpec((1, 2, 2 * NODES, width), lambda c, z: (c, z, 0, 0)),
            pl.BlockSpec((1, 1, width), lambda c, z: (c, 0, 0)),
            whole(scaling), whole(wave), whole(spread),
        ] + [whole(t) for t in tables],
        out_specs=block,
        out_shape=jax.ShapeDtypeStruct(velocity.shape, F32),
        compiler_params=pltpu.CompilerParams(vmem_limit_bytes=58 * 2**20),
        cost_estimate=pl.CostEstimate(flops=30 * 10**9, bytes_accessed=2 * 10**7, transcendentals=0),
        name="polar",
    )(velocity, far, live, scaling, wave, spread, *tables)


def polar_step(velocity, cutoff, shells, first_shell):
    comps, planes, columns, width = velocity.shape
    parts = lax.axis_size("az")
    azimuths = columns * parts
    inner_side = lax.axis_index("rad") < lax.axis_size("rad") // 2
    cutoffs = lax.dynamic_slice_in_dim(cutoff, first_shell, width)
    shell_ids = first_shell + jnp.arange(width, dtype=jnp.int32)
    live = (shell_ids[None, None, :] < shells[:, None, None]).astype(F32)
    spread, gather = cross_tables(azimuths, parts)
    g_hi, g_lo = split_table(jnp.asarray(gather))
    table = jnp.concatenate([g_hi, g_lo], axis=1)
    s_hi, s_lo = split_table(jnp.asarray(spread))
    spread_table = jnp.concatenate([s_hi, s_hi, s_lo], axis=1)
    away = jnp.arange(1, parts, dtype=jnp.int32)
    turned = (away[:, None] * (2 * cutoffs[None, :] + 1) % (2 * parts)).astype(F32) * (math.pi / parts)
    turn = jnp.stack([jnp.cos(turned), jnp.sin(turned)], axis=1)
    far_shape = (parts - 1, comps, planes, 2 * NODES, width)

    def gather_far(v):
        wave, _, _ = polar_tables(cutoffs, columns, azimuths)
        return moments(v, wave, turn, table)

    sent = lax.cond(inner_side, gather_far, lambda v: jnp.zeros(far_shape, F32), velocity)
    far = shift_from(sent[0], "az", 1)
    for n in range(1, parts - 1):
        far = far + shift_from(sent[n], "az", n + 1)

    def apply(v, f):
        wave, fourier, scaling = polar_tables(cutoffs, columns, azimuths)
        return filtered_of(v, f, live, scaling, wave, spread_table, fourier)

    return lax.cond(inner_side, apply, lambda v, f: v, velocity, far)


def local(velocity, cutoff, shells):
    _, planes, columns, radial = velocity.shape
    azimuths = columns * lax.axis_size("az")
    surface_cells = planes * lax.axis_size("ax") * azimuths
    first_shell = lax.axis_index("rad") * radial
    shell_pos = first_shell.astype(F32) + jnp.arange(radial, dtype=F32) + 0.5
    spacing = spacing_of(shell_pos, azimuths)
    scale_sq = jnp.power(spacing, 2.0 / 3.0)

    filtered = polar_step(velocity, cutoff, shells, first_shell)

    low_z = shift_from(velocity[:, -2:], "ax", -1)
    high_z = shift_from(velocity[:, :2], "ax", 1)
    tall = jnp.concatenate([low_z, velocity, high_z], axis=1)
    low_t = shift_from(tall[:, :, -PAD:], "az", -1)
    high_t = shift_from(tall[:, :, :PAD], "az", 1)
    padded = jnp.concatenate([low_t, tall, high_t], axis=2)
    inside = padded[:, 1:-1]
    lower = shift_from(inside[..., -1], "rad", -1, False)[..., None]
    upper = shift_from(inside[..., 0], "rad", 1, False)[..., None]
    lane = jnp.arange(radial)
    edges = jnp.where(lane == 0, lower, jnp.where(lane == radial - 1, upper, 0.0))
    lanes = jnp.zeros((8, radial), F32)
    lanes = lanes.at[0].set(1.0 / shell_pos).at[1].set(0.5 / spacing).at[2].set(2.0 * scale_sq)
    magnitude, sums = stencil(padded, edges, lanes)

    totals = lax.psum(jnp.sum(sums, axis=1), ("az", "ax"))
    coefficient = totals[0] / surface_cells / (totals[1] / surface_cells + 1e-06)
    viscosity = coefficient * scale_sq * magnitude[1:-1, 8:-8]
    return (filtered, viscosity, coefficient)


def solution(mesh):
    in_specs = (P(None, "ax", "az", "rad"), P(), P())
    out_specs = (P(None, "ax", "az", "rad"), P("ax", "az", "rad"), P("rad"))
    return jax.shard_map(local, mesh=mesh, in_specs=in_specs, out_specs=out_specs, check_vma=False)
```

```python
import functools
import math

import jax
import jax.numpy as jnp
import numpy as np
from jax import lax
from jax.experimental import pallas as pl
from jax.experimental.pallas import tpu as pltpu
from jax.sharding import PartitionSpec as P

MODES = 512
NODES = 48
PAD = 16
CHUNK = 16
F32 = jnp.float32
BF16 = jnp.bfloat16
PAIRS = ((0, 0), (1, 1), (2, 2), (0, 1), (0, 2), (1, 2))


def shift_from(block, axis, step, periodic=True):
    count = lax.axis_size(axis)
    pairs = [((i + step) % count, i) for i in range(count) if periodic or 0 <= i + step < count]
    return lax.ppermute(block, axis, pairs)


def spacing_of(shell_pos, azimuths):
    return jnp.maximum(shell_pos * (2.0 * math.pi / azimuths), 1.0)


def columns_kernel(x_ref, pick_ref, out_ref):
    for z in range(x_ref.shape[1]):
        out_ref[0, z] = lax.dot_general(
            pick_ref[...], x_ref[0, z], (((1,), (1,)), ((), ())),
            precision=lax.Precision.HIGHEST, preferred_element_type=F32,
        )


def outer_columns(velocity, pick):
    comps, planes, rows, width = velocity.shape
    return pl.pallas_call(
        columns_kernel,
        grid=(comps, planes // 4),
        in_specs=[
            pl.BlockSpec((1, 4, rows, width), lambda c, z: (c, z, 0, 0)),
            pl.BlockSpec((8, width), lambda c, z: (0, 0)),
        ],
        out_specs=pl.BlockSpec((1, 4, 8, rows), lambda c, z: (c, z, 0, 0)),
        out_shape=jax.ShapeDtypeStruct((comps, planes, 8, rows), F32),
        name="columns",
    )(velocity, pick)


def stencil_kernel(rows, planes, low_ref, main_ref, high_ref, left_ref, right_ref, edge_in,
                   lane_ref, pick_ref, mag_ref, sums_ref, ring, edge_ref, prev_q, prev_h, full):
    step = pl.program_id(0)
    inv_pos = lane_ref[0:1, :]
    half_space = lane_ref[1:2, :]
    scale = lane_ref[2:3, :]
    lane = lax.broadcasted_iota(jnp.int32, (CHUNK, 128), 1)
    above, here_slot, below = step % 3, (step + 2) % 3, (step + 1) % 3

    @pl.when(step == 0)
    def _():
        prev_q[...] = jnp.zeros_like(prev_q)
        prev_h[...] = jnp.zeros_like(prev_h)
        sums_ref[...] = jnp.zeros_like(sums_ref)

    def take(source):
        for c in range(3):
            ring[above, c, PAD : PAD + rows, :] = source[c, 0]

    pl.when(step < 2)(lambda: take(low_ref))
    pl.when((step >= 2) & (step < planes + 2))(lambda: take(main_ref))
    pl.when(step >= planes + 2)(lambda: take(high_ref))
    for c in range(3):
        ring[above, c, :PAD, :] = left_ref[c, 0]
        ring[above, c, PAD + rows :, :] = right_ref[c, 0]
        spread = lax.dot_general(
            edge_in[c, 0], pick_ref[...], (((0,), (0,)), ((), ())),
            precision=lax.Precision.HIGHEST, preferred_element_type=F32,
        )
        edge_ref[c] = spread[128 - PAD : 128 + rows + PAD]

    def produce(i, carry):
        base = pl.multiple_of(i * CHUNK, 8)
        here = pl.ds(base + 8, CHUNK)
        out = pl.ds(base, CHUNK)
        v, dz, dt, dr = [], [], [], []
        for c in range(3):
            wide = ring[here_slot, c, pl.ds(base, CHUNK + 16), :]
            mid = wide[8 : 8 + CHUNK]
            edge = edge_ref[c, here, :]
            v.append(mid)
            dt.append((wide[9 : 9 + CHUNK] - wide[7 : 7 + CHUNK]) * half_space)
            dz.append((ring[above, c, here, :] - ring[below, c, here, :]) * 0.5)
            up = jnp.where(lane == 127, edge, pltpu.roll(mid, 127, 1))
            down = jnp.where(lane == 0, edge, pltpu.roll(mid, 1, 1))
            dr.append((up - down) * 0.5)
        tensor = [
            dz[0],
            dr[1],
            dt[2] + v[1] * inv_pos,
            0.5 * (dr[0] + dz[1]),
            0.5 * (dt[0] + dz[2]),
            0.5 * (dr[2] - v[2] * inv_pos + dt[1]),
        ]
        diag = tensor[0] * tensor[0] + tensor[1] * tensor[1] + tensor[2] * tensor[2]
        off = tensor[3] * tensor[3] + tensor[4] * tensor[4] + tensor[5] * tensor[5]
        mag = jnp.sqrt(2.0 * diag + 4.0 * off)
        mag_ref[0, out, :] = mag
        fields = v + [v[a] * v[b] for a, b in PAIRS] + tensor + [mag * x for x in tensor]
        for f, q in enumerate(fields):
            h = prev_q[f, out, :] + q
            full[f, out, :] = prev_h[f, out, :] + h
            prev_q[f, out, :] = q
            prev_h[f, out, :] = h
        return carry

    @pl.when(step >= 2)
    def _():
        lax.fori_loop(0, (rows + 16) // CHUNK, produce, 0)

    def smoothed(f, base):
        wide = full[f, pl.ds(base, CHUNK + 16), :]
        mid = wide[8 : 8 + CHUNK]
        return (wide[7 : 7 + CHUNK] + wide[9 : 9 + CHUNK] + (mid + mid)) * 0.0625

    def consume(i, carry):
        num, den = carry
        base = pl.multiple_of(i * CHUNK, 8)
        hat_v = [smoothed(c, base) for c in range(3)]
        leo = [smoothed(3 + n, base) - hat_v[a] * hat_v[b] for n, (a, b) in enumerate(PAIRS)]
        third = (leo[0] + leo[1] + leo[2]) * (1.0 / 3.0)
        leo = [x - third for x in leo[:3]] + leo[3:]
        hat_t = [smoothed(9 + n, base) for n in range(6)]
        diag = hat_t[0] * hat_t[0] + hat_t[1] * hat_t[1] + hat_t[2] * hat_t[2]
        off = hat_t[3] * hat_t[3] + hat_t[4] * hat_t[4] + hat_t[5] * hat_t[5]
        four_mag = 4.0 * jnp.sqrt(2.0 * diag + 4.0 * off)
        lm_d = lm_o = mm_d = mm_o = 0.0
        for n in range(6):
            model = (smoothed(15 + n, base) - four_mag * hat_t[n]) * scale
            lm, mm = leo[n] * model, model * model
            if n < 3:
                lm_d, mm_d = lm_d + lm, mm_d + mm
            else:
                lm_o, mm_o = lm_o + lm, mm_o + mm
        return (num + (lm_d + 2.0 * lm_o), den + (mm_d + 2.0 * mm_o))

    @pl.when(step >= 4)
    def _():
        zero = jnp.zeros((CHUNK, 128), F32)
        num, den = lax.fori_loop(0, rows // CHUNK, consume, (zero, zero))
        sums_ref[0] += num
        sums_ref[1] += den


def stencil(low, velocity, high, left, right, edges, lanes, pick):
    _, planes, rows, width = velocity.shape
    steps = planes + 4
    block = (3, 1, rows, width)
    side = pl.BlockSpec((3, 1, PAD, width), lambda j: (0, j, 0, 0))
    small = pl.BlockSpec((8, width), lambda j: (0, 0))
    return pl.pallas_call(
        functools.partial(stencil_kernel, rows, planes),
        grid=(steps,),
        in_specs=[
            pl.BlockSpec(block, lambda j: (0, jnp.clip(j, 0, 1), 0, 0)),
            pl.BlockSpec(block, lambda j: (0, jnp.clip(j - 2, 0, planes - 1), 0, 0)),
            pl.BlockSpec(block, lambda j: (0, jnp.clip(j - planes - 2, 0, 1), 0, 0)),
            side,
            side,
            pl.BlockSpec((3, 1, 8, edges.shape[3]), lambda j: (0, jnp.clip(j - 2, 0, planes + 1), 0, 0)),
            small,
            small,
        ],
        out_specs=[
            pl.BlockSpec((1, rows + 16, width), lambda j: (jnp.clip(j - 2, 0, planes + 1), 0, 0)),
            pl.BlockSpec((2, CHUNK, width), lambda j: (0, 0, 0)),
        ],
        out_shape=[
            jax.ShapeDtypeStruct((planes + 2, rows + 16, width), F32),
            jax.ShapeDtypeStruct((2, CHUNK, width), F32),
        ],
        scratch_shapes=[
            pltpu.VMEM((3, 3, rows + 2 * PAD, width), F32),
            pltpu.VMEM((3, rows + 2 * PAD, width), F32),
        ] + [pltpu.VMEM((21, rows + 16, width), F32)] * 3,
        compiler_params=pltpu.CompilerParams(vmem_limit_bytes=58 * 2**20),
        cost_estimate=pl.CostEstimate(flops=10**9, bytes_accessed=10**8, transcendentals=0),
        name="stencil",
    )(low, velocity, high, left, right, edges, lanes, pick)


def split(x):
    high = x.astype(BF16)
    return high, (x - high.astype(F32)).astype(BF16)


def split_table(x):
    high = lax.reduce_precision(x, 8, 7)
    return high.astype(BF16), (x - high).astype(BF16)


def mm(a, b):
    return jnp.dot(a, b, preferred_element_type=F32)


def cross_tables(azimuths, parts):
    local = azimuths // parts
    pos = math.pi * (np.arange(local) - (local - 1) / 2.0) / azimuths
    edge = math.tan(math.pi * local / (2.0 * azimuths)) if parts > 1 else 1.0
    ratio = np.tan(pos) / edge
    var = np.log((1.0 + ratio) / (1.0 - ratio))
    reach = var[-1]
    theta = (np.arange(NODES) + 0.5) * math.pi / NODES
    nodes = reach * np.cos(theta)
    node_pos = np.arctan(edge * np.tanh(nodes / 2.0))
    weight = np.sin(theta) * (-1.0) ** np.arange(NODES)
    gap = var[:, None] - nodes[None, :]
    gap = np.where(np.abs(gap) < 1e-13, 1e-13, gap)
    lag = weight[None, :] / gap
    lag = lag / np.sum(lag, axis=1, keepdims=True)
    spread = lag / np.cos(pos)[:, None]
    gather = []
    for away in range(1, parts):
        source = pos + math.pi * local * away / azimuths
        gather.append(np.cos(node_pos)[:, None] / np.sin(node_pos[:, None] - source[None, :]) / azimuths)
    return spread.astype(np.float32), np.stack(gather).astype(np.float32)


def twice(x):
    return jnp.concatenate([x, x], axis=1)


def moment_kernel(x_ref, wave_ref, turn_ref, table_ref, out_ref):
    x = jnp.concatenate([x_ref[0, 0], x_ref[0, 1]], axis=1)
    c_hi, c_lo = split(x * twice(wave_ref[0]))
    s_hi, s_lo = split(x * twice(wave_ref[1]))
    for away in range(table_ref.shape[0]):
        table = table_ref[away]

        def apply(high, low):
            both = mm(table, high)
            return both[:NODES] + (both[NODES:] + mm(table[:NODES], low))

        by_cos, by_sin = apply(c_hi, c_lo), apply(s_hi, s_lo)
        cos_turn = twice(turn_ref[away, 0:1])
        sin_turn = twice(turn_ref[away, 1:2])
        first = by_cos * cos_turn - by_sin * sin_turn
        second = by_sin * cos_turn + by_cos * sin_turn
        for k in range(2):
            cols = slice(128 * k, 128 * k + 128)
            out_ref[away, 0, k, :NODES] = first[:, cols]
            out_ref[away, 0, k, NODES:] = second[:, cols]


def filter_kernel(x_ref, far_ref, live_ref, scaling_ref, wave_ref, spread_ref,
                  fwd_hi, fwd_lo, inv_hi, inv_lo, out_ref):
    x = jnp.concatenate([x_ref[0, 0], x_ref[0, 1]], axis=1)
    x_hi, x_lo = split(x)
    spectrum = mm(fwd_hi[...], x_hi) + (mm(fwd_hi[...], x_lo) + mm(fwd_lo[...], x_hi))
    s_hi, s_lo = split(spectrum * twice(scaling_ref[...]))
    near = mm(inv_hi[...], s_hi) + (mm(inv_hi[...], s_lo) + mm(inv_lo[...], s_hi))
    far = jnp.concatenate([far_ref[0, 0], far_ref[0, 1]], axis=1)
    f_hi, f_lo = split(far)

    def spread(rows):
        stacked = jnp.concatenate([f_hi[rows], f_lo[rows], f_hi[rows]], axis=0)
        return mm(spread_ref[...], stacked)

    by_cos = spread(slice(0, NODES))
    by_sin = spread(slice(NODES, 2 * NODES))
    result = near + (twice(wave_ref[1]) * by_cos - twice(wave_ref[0]) * by_sin)
    result = jnp.where(twice(live_ref[0]) > 0.5, result, x)
    out_ref[0, 0] = result[:, :128]
    out_ref[0, 1] = result[:, 128:]


def polar_tables(cutoffs, columns, azimuths):
    order = 2 * cutoffs + 1
    offset = 2 * jnp.arange(columns, dtype=jnp.int32) - (columns - 1)
    unit = math.pi / (2.0 * azimuths)
    phase = (offset[:, None] * order[None, :] % (4 * azimuths)).astype(F32) * unit
    wave = jnp.stack([jnp.cos(phase), jnp.sin(phase)])
    modes = jnp.arange(MODES, dtype=jnp.int32)
    angle = (2 * offset[None, :] * modes[:, None] % (4 * azimuths)).astype(F32) * unit
    fourier = jnp.concatenate([jnp.cos(angle), jnp.sin(angle)], axis=0)
    weight = jnp.where(modes == 0, 1.0, 2.0).astype(F32) / azimuths
    kept = jnp.where(modes[:, None] <= cutoffs[None, :], weight[:, None], 0.0)
    return wave, fourier, jnp.concatenate([kept, kept], axis=0)


def moments(velocity, wave, turn, table):
    comps, planes, columns, width = velocity.shape
    far = table.shape[0]
    return pl.pallas_call(
        moment_kernel,
        grid=(comps, planes // 2),
        in_specs=[
            pl.BlockSpec((1, 2, columns, width), lambda c, z: (c, z, 0, 0)),
            pl.BlockSpec(wave.shape, lambda c, z: (0, 0, 0)),
            pl.BlockSpec(turn.shape, lambda c, z: (0, 0, 0)),
            pl.BlockSpec(table.shape, lambda c, z: (0, 0, 0)),
        ],
        out_specs=pl.BlockSpec((far, 1, 2, 2 * NODES, width), lambda c, z: (0, c, z, 0, 0)),
        out_shape=jax.ShapeDtypeStruct((far, comps, planes, 2 * NODES, width), F32),
        name="moments",
    )(velocity, wave, turn, table)


def filtered_of(velocity, far, live, scaling, wave, spread, fourier):
    comps, planes, columns, width = velocity.shape
    tables = fourier

    def whole(x):
        return pl.BlockSpec(x.shape, lambda c, z: (0,) * x.ndim, pipeline_mode=pl.Buffered(1))

    block = pl.BlockSpec((1, 2, columns, width), lambda c, z: (c, z, 0, 0))
    return pl.pallas_call(
        filter_kernel,
        grid=(comps, planes // 2),
        in_specs=[
            block,
            pl.BlockSpec((1, 2, 2 * NODES, width), lambda c, z: (c, z, 0, 0)),
            pl.BlockSpec((1, 1, width), lambda c, z: (c, 0, 0)),
            whole(scaling), whole(wave), whole(spread),
        ] + [whole(t) for t in tables],
        out_specs=block,
        out_shape=jax.ShapeDtypeStruct(velocity.shape, F32),
        compiler_params=pltpu.CompilerParams(vmem_limit_bytes=58 * 2**20),
        cost_estimate=pl.CostEstimate(flops=30 * 10**9, bytes_accessed=2 * 10**7, transcendentals=0),
        name="polar",
    )(velocity, far, live, scaling, wave, spread, *tables)


def polar_step(velocity, cutoff, shells, first_shell):
    comps, planes, columns, width = velocity.shape
    parts = lax.axis_size("az")
    azimuths = columns * parts
    inner_side = lax.axis_index("rad") < lax.axis_size("rad") // 2
    cutoffs = lax.dynamic_slice_in_dim(cutoff, first_shell, width)
    shell_ids = first_shell + jnp.arange(width, dtype=jnp.int32)
    live = (shell_ids[None, None, :] < shells[:, None, None]).astype(F32)
    spread, gather = cross_tables(azimuths, parts)
    g_hi, g_lo = split_table(jnp.asarray(gather))
    table = jnp.concatenate([g_hi, g_lo], axis=1)
    s_hi, s_lo = split_table(jnp.asarray(spread))
    spread_table = jnp.concatenate([s_hi, s_hi, s_lo], axis=1)
    away = jnp.arange(1, parts, dtype=jnp.int32)
    turned = (away[:, None] * (2 * cutoffs[None, :] + 1) % (2 * parts)).astype(F32) * (math.pi / parts)
    turn = jnp.stack([jnp.cos(turned), jnp.sin(turned)], axis=1)
    far_shape = (parts - 1, comps, planes, 2 * NODES, width)

    wave, fourier, scaling = polar_tables(cutoffs, columns, azimuths)
    sent = lax.cond(
        inner_side,
        lambda v: moments(v, wave, turn, table),
        lambda v: jnp.zeros(far_shape, F32),
        velocity,
    )
    far = shift_from(sent[0], "az", 1)
    for n in range(1, parts - 1):
        far = far + shift_from(sent[n], "az", n + 1)
    fwd_hi, fwd_lo = split_table(fourier)
    tables = (fwd_hi, fwd_lo, fwd_hi.T, fwd_lo.T)
    return lax.cond(
        inner_side,
        lambda v, f: filtered_of(v, f, live, scaling, wave, spread_table, tables),
        lambda v, f: v,
        velocity,
        far,
    )


def local(velocity, cutoff, shells):
    _, planes, columns, radial = velocity.shape
    azimuths = columns * lax.axis_size("az")
    surface_cells = planes * lax.axis_size("ax") * azimuths
    first_shell = lax.axis_index("rad") * radial
    shell_pos = first_shell.astype(F32) + jnp.arange(radial, dtype=F32) + 0.5
    spacing = spacing_of(shell_pos, azimuths)
    scale_sq = jnp.power(spacing, 2.0 / 3.0)

    left = shift_from(velocity[:, :, -PAD:], "az", -1)
    right = shift_from(velocity[:, :, :PAD], "az", 1)
    low = shift_from(velocity[:, -2:], "ax", -1)
    high = shift_from(velocity[:, :2], "ax", 1)

    pick = np.zeros((8, radial), np.float32)
    pick[0, 0] = pick[1, radial - 1] = 1.0
    pick = jnp.asarray(pick)
    columns_out = outer_columns(velocity, pick)
    lower = shift_from(columns_out[:, :, 1:2], "rad", -1, False)
    upper = shift_from(columns_out[:, :, 0:1], "rad", 1, False)
    edges = jnp.concatenate([lower, upper, jnp.zeros((3, planes, 6, columns), F32)], axis=2)
    edges = jnp.concatenate(
        [shift_from(edges[..., -128:], "az", -1), edges, shift_from(edges[..., :128], "az", 1)], axis=3
    )
    sides = jnp.concatenate([left, right], axis=2)
    rims = (
        low,
        high,
        shift_from(edges[:, -1:], "ax", -1),
        shift_from(edges[:, :1], "ax", 1),
        shift_from(sides[:, -2:], "ax", -1),
        shift_from(sides[:, :2], "ax", 1),
    )

    filtered = polar_step(velocity, cutoff, shells, first_shell)
    filtered, low, high, edge_low, edge_high, side_low, side_high = lax.optimization_barrier((filtered,) + rims)
    edges = jnp.concatenate([edge_low, edges, edge_high], axis=1)
    sides = jnp.concatenate([side_low, sides, side_high], axis=1)
    left, right = sides[:, :, :PAD], sides[:, :, PAD:]
    lanes = jnp.zeros((8, radial), F32)
    lanes = lanes.at[0].set(1.0 / shell_pos).at[1].set(0.5 / spacing).at[2].set(2.0 * scale_sq)
    magnitude, sums = stencil(low, velocity, high, left, right, edges, lanes, pick)

    totals = lax.psum(jnp.sum(sums, axis=1), ("az", "ax"))
    coefficient = totals[0] / surface_cells / (totals[1] / surface_cells + 1e-06)
    viscosity = coefficient * scale_sq * magnitude[1:-1, 8:-8]
    return (filtered, viscosity, coefficient)


def solution(mesh):
    in_specs = (P(None, "ax", "az", "rad"), P(), P())
    out_specs = (P(None, "ax", "az", "rad"), P("ax", "az", "rad"), P("rad"))
    return jax.shard_map(local, mesh=mesh, in_specs=in_specs, out_specs=out_specs, check_vma=False)
```
